32 devices in a mesh: nodes: 8 (over z, y), mp: 4 (over x, core).
Axes of the slice: x: 2, y: 2, z: 4, core: 2. Of those that a mesh axis runs over, the one named last changes fastest.
Arguments:
- query: bfloat16 [2048, 512], P('nodes', 'mp'), may hold values from -240 to 240
- key: bfloat16 [2048, 512], P('nodes', 'mp'), may hold values from -7 to 7
- value: bfloat16 [2048, 512], P('nodes', 'mp'), may hold values from -12 to 12
- out_weight: bfloat16 [512, 512], P('mp'), may hold values from -0.25 to 0.25
- cotangent: bfloat16 [2048, 512], P('nodes', 'mp'), may hold values from -6 to 6
- virtual_key: bfloat16 [64, 512], P('nodes', 'mp'), may hold values from -6 to 6
- virtual_value: bfloat16 [64, 512], P('nodes', 'mp'), may hold values from -12 to 12
- halo_rows: int32 [8, 2, 128], P('nodes'), may hold values from 0 to 255
- halo_live: int32 [8, 2], P('nodes'), may hold values from 64 to 128, as said below
- expand_rows: int32 [8, 8, 2], P('nodes'), may hold values from 0 to 255
- local_mask: int32 [16, 4], P('nodes'), may hold values from 0 to 1, as said below
- expand_mask: int32 [16, 8], P('nodes'), may hold values 0 or 1
Outputs:
- output: bfloat16 [2048, 512], P('nodes', 'mp')
- grad_query: float32 [2048, 512], P('nodes', 'mp')
- grad_key: float32 [2048, 512], P('nodes', 'mp')
- grad_value: float32 [2048, 512], P('nodes', 'mp')
- grad_virtual_key: float32 [64, 512], P('nodes', 'mp')
- grad_virtual_value: float32 [64, 512], P('nodes', 'mp')
The draws below stay inside these ranges and needn't reach their ends.
Inputs may be any that keep to these rules, and one draw needn't show every extreme that they name: halo_rows[p, 0, :] index nodes of partition p (0 to 255) sent to partition p + 1, halo_rows[p, 1, :] those sent to partition p - 1; repeats possible. Only the leading halo_live slots of what a partition receives from a neighbour are edges; the value 128 occurs in every draw. expand_rows[r, p, :] index nodes of partition r. Every query tile attends its own tile and both received boundary tiles: local_mask[t, t mod 2], local_mask[t, 2] and local_mask[t, 3] are 1.
All inputs are finite; a program needn't handle non-finite values. No bound on the sum of `expand_mask` on one device may be relied on, other than what follows from the above.
Results may differ from the reference program's by a relative error of at most 0.034.
Values may be sent and summed in bfloat16 or wider, within the bound.
A program may use at most 64 MiB of HBM per device.

```python
import jax
import jax.numpy as jnp
from jax import lax

D = 512
HEADS = 8
NODE_DEV = 256
TILE = 128
HALO_CAP = 128
EXP_SLOT = 2
VN = 64
NODES = 2048
N_NODES = 8


def pair_fields(key):
    key_field = jnp.clip(jax.random.normal(jax.random.fold_in(key, 101), (NODES, D), jnp.float32), -6.0, 6.0)
    query_field = 2.0 * jnp.clip(jax.random.normal(jax.random.fold_in(key, 102), (NODES, D), jnp.float32), -6.0, 6.0)
    return (key_field, query_field)


def draw_query(key, part):
    return pair_fields(key)[1].astype(jnp.bfloat16)


def draw_key(key, part):
    return pair_fields(key)[0].astype(jnp.bfloat16)


def draw_halo_live(key, part):
    devices = NODES // NODE_DEV
    levels = jax.random.randint(jax.random.fold_in(key, 7), (devices, 2), 0, 2)
    live = HALO_CAP // jnp.power(2, levels)
    chosen = jax.random.randint(jax.random.fold_in(key, 8), (), 0, devices * 2)
    flat_index = jnp.arange(devices * 2).reshape(devices, 2)
    return jnp.where(flat_index == chosen, HALO_CAP, live).astype(jnp.int32)


def draw_local_mask(key, part):
    tiles = NODES // TILE
    columns = NODE_DEV // TILE + 2
    random_bits = jax.random.randint(jax.random.fold_in(key, 9), (tiles, columns), 0, 2)
    tile_ids = jnp.arange(tiles)[:, None]
    column_ids = jnp.arange(columns)[None, :]
    forced = (column_ids == tile_ids % (NODE_DEV // TILE)) | (column_ids >= NODE_DEV // TILE)
    return jnp.where(forced, 1, random_bits).astype(jnp.int32)


def set_ends(drawn, stream_key, least, high):
    spot = [jax.random.randint(jax.random.fold_in(stream_key, axis), (), 0, length) for axis, length in enumerate(drawn.shape)]
    longest = drawn.shape.index(max(drawn.shape))
    neighbour = spot[:longest] + [(spot[longest] + 1) % drawn.shape[longest]] + spot[longest + 1:]
    return drawn.at[tuple(spot)].set(least).at[tuple(neighbour)].set(high)


def steps_of(own_key, dims, pieces, smallest, high):
    def one(position, shards_of):
        draws = jax.random.uniform(jax.random.fold_in(jax.random.fold_in(own_key, 6), position), (shards_of,), jnp.float32, smallest / len(pieces), high / len(pieces))
        return jnp.repeat(jnp.exp(draws), dims[position] // shards_of).reshape((-1,) + (1,) * (len(dims) - position - 1))

    level = one(*pieces[0])
    for cut in pieces[1:]:
        level = level * one(*cut)
    return level


def gaussian(own_key, extent, spread, reach, shards=(), held_as=jnp.bfloat16):
    result = jax.random.normal(own_key, extent, jnp.float32) * spread
    if len(shards) > 0:
        result = steps_of(own_key, extent, shards, -0.22, 0.18) * result
    return jnp.clip(result, min=-reach, max=reach).astype(held_as)


def setup_inputs(seed: int = 0) -> dict:
    arg_keys = jax.random.split(jax.random.key(seed), 13)
    query = draw_query(jax.random.fold_in(arg_keys[12], 71), 0)
    key = draw_key(jax.random.fold_in(arg_keys[12], 71), 0)
    value = gaussian(arg_keys[2], (NODES, D), 2.0, 12.0, ((0, 8), (1, 4)))
    out_weight = gaussian(arg_keys[3], (D, D), D ** -0.5, 0.25, ((0, 4),))
    cotangent = gaussian(arg_keys[4], (NODES, D), 1.0, 6.0, ((0, 8), (1, 4)))
    virtual_key = gaussian(arg_keys[5], (VN, D), 1.0, 6.0, ((0, 8), (1, 4)))
    virtual_value = gaussian(arg_keys[6], (VN, D), 2.0, 12.0, ((0, 8), (1, 4)))
    halo_rows = set_ends(jax.random.randint(arg_keys[7], (N_NODES, 2, HALO_CAP), 0, NODE_DEV), jax.random.fold_in(arg_keys[7], 1), 0, NODE_DEV - 1).astype(jnp.int32)
    halo_live = draw_halo_live(jax.random.fold_in(arg_keys[12], 71), 0)
    expand_rows = set_ends(jax.random.randint(arg_keys[9], (N_NODES, N_NODES, EXP_SLOT), 0, NODE_DEV), jax.random.fold_in(arg_keys[9], 1), 0, NODE_DEV - 1).astype(jnp.int32)
    local_mask = draw_local_mask(jax.random.fold_in(arg_keys[12], 71), 0)
    expand_mask = set_ends((jax.random.randint(arg_keys[11], (NODES // TILE, N_NODES), 0, 4) < 1).astype(jnp.int32), jax.random.fold_in(arg_keys[11], 1), 0, 1)
    return {"query": query, "key": key, "value": value, "out_weight": out_weight, "cotangent": cotangent, "virtual_key": virtual_key, "virtual_value": virtual_value, "halo_rows": halo_rows, "halo_live": halo_live, "expand_rows": expand_rows, "local_mask": local_mask, "expand_mask": expand_mask}


def edge_mask(local_block, expand_block, live, tile_rows, halo_cap, exp_slot, virtual_count):
    tile_count = local_block.shape[0]
    own_tiles = jnp.repeat(jnp.repeat(local_block[:, :tile_count] > 0, tile_rows, axis=0), tile_rows, axis=1)
    slot_index = jnp.arange(halo_cap)
    left_ok = (local_block[:, tile_count] > 0)[:, None] & (slot_index < live[0])[None, :]
    right_ok = (local_block[:, tile_count + 1] > 0)[:, None] & (slot_index < live[1])[None, :]
    expand_ok = jnp.repeat(expand_block > 0, exp_slot, axis=1)
    remote_tiles = jnp.repeat(jnp.concatenate([left_ok, right_ok, expand_ok], axis=1), tile_rows, axis=0)
    virtual_ok = jnp.ones((tile_count * tile_rows, virtual_count), dtype=jnp.bool_)
    return jnp.concatenate([own_tiles, remote_tiles, virtual_ok], axis=1)


def reference(query, key, value, out_weight, cotangent, virtual_key, virtual_value, halo_rows, halo_live, expand_rows, local_mask, expand_mask):
    node_rows = NODE_DEV
    part_count = N_NODES
    tile_count = NODE_DEV // TILE
    head_dim = D // HEADS
    score_scale = head_dim ** -0.5
    part_ids = jnp.arange(part_count, dtype=jnp.int32)
    left_part = (part_ids - 1) % part_count
    right_part = (part_ids + 1) % part_count
    left_index = left_part[:, None] * node_rows + halo_rows[left_part, 0]
    right_index = right_part[:, None] * node_rows + halo_rows[right_part, 1]
    expand_index = (part_ids[:, None, None] * node_rows + expand_rows).transpose(1, 0, 2).reshape(part_count, part_count * EXP_SLOT)
    own_index = part_ids[:, None] * node_rows + jnp.arange(node_rows, dtype=jnp.int32)[None, :]
    key_index = jnp.concatenate([own_index, left_index, right_index, expand_index], axis=1).astype(jnp.int32)
    local_keys = key_index.shape[1]

    def block_step(carry, part):
        grad_key_all, grad_value_all, virtual_key_grad, virtual_value_grad = carry
        row_start = (part * node_rows).astype(jnp.int32)
        tile_start = (part * tile_count).astype(jnp.int32)
        block_query = lax.dynamic_slice_in_dim(query, row_start, node_rows, 0)
        block_cot = lax.dynamic_slice_in_dim(cotangent, row_start, node_rows, 0)
        block_local = lax.dynamic_slice_in_dim(local_mask, tile_start, tile_count, 0)
        block_expand = lax.dynamic_slice_in_dim(expand_mask, tile_start, tile_count, 0)
        gather_index = key_index[part]
        all_keys = jnp.concatenate([key[gather_index], virtual_key], axis=0)
        all_values = jnp.concatenate([value[gather_index], virtual_value], axis=0)
        key_total = all_keys.shape[0]
        allowed = edge_mask(block_local, block_expand, halo_live[part], TILE, HALO_CAP, EXP_SLOT, VN)
        query_heads = block_query.astype(jnp.float32).reshape(node_rows, HEADS, head_dim)
        key_heads = all_keys.astype(jnp.float32).reshape(key_total, HEADS, head_dim)
        value_heads = all_values.astype(jnp.float32).reshape(key_total, HEADS, head_dim)
        scores = jnp.einsum('qhd,khd->hqk', query_heads, key_heads) * score_scale
        scores = jnp.where(allowed[None], scores, -1e30)
        row_max = jnp.max(scores, axis=-1, keepdims=True)
        weights = jnp.exp(scores - row_max)
        probs = weights / jnp.sum(weights, axis=-1, keepdims=True)
        probs_b = lax.optimization_barrier(probs.astype(jnp.bfloat16)).astype(jnp.float32)
        attn = jnp.einsum('hqk,khd->qhd', probs_b, value_heads).astype(jnp.bfloat16).reshape(node_rows, D)
        output_block = jnp.dot(attn, out_weight, preferred_element_type=jnp.float32).astype(jnp.bfloat16)
        d_attn = jnp.dot(block_cot, out_weight.T, preferred_element_type=jnp.float32).astype(jnp.bfloat16)
        grad_heads = d_attn.astype(jnp.float32).reshape(node_rows, HEADS, head_dim)
        attn_heads = attn.astype(jnp.float32).reshape(node_rows, HEADS, head_dim)
        row_delta = jnp.sum(grad_heads * attn_heads, axis=-1).transpose(1, 0)[:, :, None]
        d_prob = jnp.einsum('qhd,khd->hqk', grad_heads, value_heads)
        d_score = lax.optimization_barrier((probs * (d_prob - row_delta) * score_scale).astype(jnp.bfloat16)).astype(jnp.float32)
        grad_query_block = jnp.einsum('hqk,khd->qhd', d_score, key_heads).reshape(node_rows, D)
        grad_keys = jnp.einsum('hqk,qhd->khd', d_score, query_heads).reshape(key_total, D)
        grad_values = jnp.einsum('hqk,qhd->khd', probs_b, grad_heads).reshape(key_total, D)
        grad_key_all = grad_key_all.at[gather_index].add(grad_keys[:local_keys])
        grad_value_all = grad_value_all.at[gather_index].add(grad_values[:local_keys])
        virtual_key_grad = virtual_key_grad + grad_keys[local_keys:]
        virtual_value_grad = virtual_value_grad + grad_values[local_keys:]
        return (grad_key_all, grad_value_all, virtual_key_grad, virtual_value_grad), (output_block, grad_query_block)

    start_carry = (jnp.zeros((NODES, D), jnp.float32), jnp.zeros((NODES, D), jnp.float32), jnp.zeros((VN, D), jnp.float32), jnp.zeros((VN, D), jnp.float32))
    final_carry, stacked = lax.scan(block_step, start_carry, part_ids)
    grad_key_all, grad_value_all, virtual_key_grad, virtual_value_grad = final_carry
    output = stacked[0].reshape(NODES, D)
    grad_query = stacked[1].reshape(NODES, D)
    return (output, grad_query, grad_key_all, grad_value_all, virtual_key_grad, virtual_value_grad)
```

```python
import functools

import jax
import jax.numpy as jnp
from jax import lax
from jax.experimental import pallas as pl
from jax.experimental.pallas import tpu as pltpu
from jax.sharding import PartitionSpec as P

HEADS = 8
MESH = pl.DeviceIdType.MESH
BF = jnp.bfloat16
F32 = jnp.float32
MASKED = -1e30

NN = (((1,), (0,)), ((), ()))
NT = (((1,), (1,)), ((), ()))
TN = (((0,), (0,)), ((), ()))


def mm(a, b, dims):
    return lax.dot_general(a, b, dims, preferred_element_type=F32)


def iota(shape, axis):
    return lax.broadcasted_iota(jnp.int32, shape, axis)


def each(count, step):
    if count <= 8:
        for d in range(count):
            step(d)
    else:
        pl.loop(0, count)(step)


def kernel(
    n, mp, heads,
    live_hbm, erows_hbm, lmask_hbm, emask_hbm,
    q_hbm, k_hbm, v_hbm, w_hbm, cot_hbm, vk_hbm, vv_hbm, hrows_hbm,
    out_v, gq_v, gk_v, gv_v, gvk_v, gvv_v,
    live, erows, lmask, emask, q_v, w_v, vkv, hrows, kv, cot, bias, picks, send_buf,
    kvt, e_ref, dp_ref, pb_ref, ds_ref, gback, ret, proj, proj_in,
    in_sem, in_nodes, in_mp, near_r, far_r, out_s, cot_s, cot_r, proj_s, proj_r, home_s, home_near_r, home_far_r,
):
    me = lax.axis_index("nodes")
    mm_i = lax.axis_index("mp")
    rows, width = q_v.shape
    tiles = lmask.shape[0]
    tile = rows // tiles
    cap = hrows.shape[2]
    slots = erows.shape[1]
    vn = vkv.shape[1]
    mix = ret.shape[0] - 2 * cap
    blk = mix // n
    hd = width // heads
    cols = heads * rows
    odd = lax.rem(me, 2)
    left, right = lax.rem(me + n - 1, n), lax.rem(me + 1, n)
    near = jnp.where(odd == 0, right, left)
    far = jnp.where(odd == 0, left, right)
    far0 = rows + cap
    mix0 = rows + 2 * cap
    total = mix0 + mix
    bands = in_nodes.shape[0] - 1
    band = n // bands

    barrier = pltpu.get_barrier_semaphore()

    def greet(sem, **device):
        pl.semaphore_signal(sem, inc=1, device_id=device, device_id_type=MESH)

    half, end = n // 2, n - 1
    pl.loop(me + 1, jnp.where(me >= half, end, n))(lambda j: greet(barrier, nodes=j))
    pl.when(me == end)(lambda: pl.loop(half, end)(lambda j: greet(barrier, nodes=j)))

    def swap(j):
        return j + 1 - 2 * lax.rem(j, 2) if mp % 2 == 0 else j

    spot = swap(mm_i)
    pl.loop(spot + 1, mp)(lambda j: greet(barrier, mp=swap(j)))

    def load(i, src, dst):
        return pltpu.make_async_copy(src, dst, in_sem.at[i])

    kv_in = [load(0, k_hbm, kv.at[:rows, :width]), load(0, v_hbm, kv.at[:rows, width:])]
    hrows_in = load(1, hrows_hbm, hrows)
    erows_in = load(2, erows_hbm, erows)
    vkv_in = [load(3, vk_hbm, vkv.at[0]), load(3, vv_hbm, vkv.at[1])]
    cot_in = load(4, cot_hbm, cot.at[mm_i])
    q_in = load(5, q_hbm, q_v)
    w_in = load(6, w_hbm, w_v)
    small = [load(7, live_hbm, live), load(8, lmask_hbm, lmask), load(9, emask_hbm, emask)]
    for c in [erows_in, *kv_in, hrows_in]:
        c.start()

    lower = jnp.where(me == end, half, me)
    expected = lower + jnp.where((me >= half) & (me < end), 1, 0)

    def await_all(sem, count):
        pl.when(count > 0)(lambda: pl.semaphore_wait(sem, count))

    await_all(barrier, expected + spot)
    mine_in = jnp.where(me == end, bands, me // band)
    pl.loop(0, lower)(lambda j: greet(in_nodes.at[mine_in], nodes=j))
    pl.when((me >= half) & (me < end))(lambda: greet(in_nodes.at[mine_in], nodes=end))
    pl.loop(0, spot)(lambda j: greet(in_mp.at[0], mp=swap(j)))
    for c in [*vkv_in, cot_in, q_in, w_in, *small]:
        c.start()

    groups = mix // cap
    place = iota((groups, cap), 0) * cap + iota((groups, cap), 1)

    def pick_mix(d, target):
        peer = lax.rem(me + d, n)
        for s in range(slots):
            target = jnp.where(place == d * blk + vn + s, erows[0, s, peer], target)
        return target

    erows_in.wait()
    target = jnp.full((groups, cap), -1, jnp.int32)
    if n <= 8:
        for d in range(n):
            target = pick_mix(d, target)
    else:
        target = lax.fori_loop(0, n, pick_mix, target)

    hrows_in.wait()
    near_rows = jnp.where(odd == 0, hrows[0, 0:1, :], hrows[0, 1:2, :])
    far_rows = jnp.where(odd == 0, hrows[0, 1:2, :], hrows[0, 0:1, :])
    wanted = jnp.concatenate([near_rows, far_rows, target], axis=0)
    lines = 2 + groups
    padded = -(-lines // 8) * 8
    columns = jnp.concatenate(
        [wanted.astype(F32), jnp.zeros((padded - lines, cap), F32)], axis=0
    )
    columns = jnp.transpose(columns).astype(jnp.int32)
    lane_p = iota((cap, rows), 1)
    for i in range(lines):
        picks[i * cap : (i + 1) * cap, :] = jnp.where(
            lane_p == columns[:, i : i + 1], 1.0, 0.0
        ).astype(BF)

    load(0, kv.at[:rows, :], kv.at[:rows, :]).wait()
    own = kv[:rows, :]
    taken = mm(picks[...], own, NN)
    load(3, vkv, vkv).wait()
    virt = jnp.concatenate([vkv[0].astype(F32), vkv[1].astype(F32)], axis=1)
    virt = jnp.concatenate([virt, jnp.zeros((blk - vn, 2 * width), F32)], axis=0)
    send_buf[: 2 * cap, :] = taken[: 2 * cap].astype(BF)
    mixed = (taken[2 * cap :].reshape(n, blk, 2 * width) + virt[None]).astype(BF)
    send_buf[2 * cap :, :] = mixed.reshape(mix, 2 * width)
    cot_in.wait()

    def push(src, dst, send, recv, **device):
        return pltpu.make_async_remote_copy(
            src, dst, send.at[0], recv.at[0], device_id=device, device_id_type=MESH
        )

    def mix_copy(d):
        return push(
            send_buf.at[pl.ds(2 * cap + d * blk, blk), :], kv.at[pl.ds(mix0 + d * blk, blk), :],
            out_s, far_r, nodes=lax.rem(me + d, n),
        )

    def cot_copy(d):
        return push(cot.at[mm_i], cot.at[mm_i], cot_s, cot_r, mp=lax.rem(mm_i + d, mp))

    def far_copy():
        push(send_buf.at[cap : 2 * cap, :], kv.at[far0:mix0, :], out_s, far_r, nodes=far).start()

    def near_copy():
        push(send_buf.at[:cap, :], kv.at[rows:far0, :], out_s, near_r, nodes=near).start()

    def send_mix(peer):
        pl.when(peer != me)(lambda: mix_copy(lax.rem(peer - me + n, n)).start())

    def send_cot():
        await_all(in_mp.at[0], mp - 1 - spot)
        for d in range(1, mp):
            cot_copy(d).start()

    early = me < half
    pl.when(early)(send_cot)
    for g in range(bands):
        if g == bands // 2:

            @pl.when(early)
            def _():
                pl.semaphore_wait(in_nodes.at[bands], 1)
                pl.when(far == end)(far_copy)
                send_mix(end)

        above = jnp.where(me == end, half, me + 1)
        above = jnp.maximum(g * band, above)
        await_all(in_nodes.at[g], min((g + 1) * band, end) - above)
        pl.when((far // band == g) & ((far < end) | (me >= half)))(far_copy)
        pl.when(near // band == g)(near_copy)
        each(min(band, end - g * band), lambda j: send_mix(g * band + j))
    pl.when(me >= half)(lambda: send_mix(end))
    pl.when(me >= half)(send_cot)
    kv[mix0 : mix0 + blk, :] = send_buf[2 * cap : 2 * cap + blk, :]
    for c in small:
        c.wait()

    lane = iota((1, width), 1)

    def per_tile(values):
        result = jnp.zeros(values[0].shape, F32)
        for t in range(tiles):
            result = jnp.where(lane == t, values[t], result)
        return result.astype(BF)

    def flag(x):
        return jnp.where(x > 0, 0.0, MASKED)

    for u in range(tiles):
        bias[u * tile : (u + 1) * tile, :] = per_tile(
            [jnp.full((tile, width), flag(lmask[t, u]), F32) for t in range(tiles)]
        )
    row_c = iota((cap, width), 0)
    for start, side in ((rows, 1 - odd), (far0, odd)):
        bias[start : start + cap, :] = per_tile(
            [
                jnp.where(row_c < live[0, side], flag(lmask[t, tiles + side]), MASKED)
                for t in range(tiles)
            ]
        )
    row_m = iota((blk, width), 0)

    def mix_mask(d):
        source = lax.rem(me + n - d, n)
        values = []
        for t in range(tiles):
            inner = jnp.where(row_m < vn + slots, flag(emask[t, source]), MASKED)
            values.append(jnp.where(row_m < vn, 0.0, inner))
        bias[pl.ds(mix0 + d * blk, blk), :] = per_tile(values)

    each(n, mix_mask)

    feature = iota((width, rows), 0)

    def blocks(x):
        parts = []
        for h in range(heads):
            mine = (feature >= h * hd) & (feature < (h + 1) * hd)
            parts.append(jnp.where(mine, x, 0.0))
        return jnp.concatenate(parts, axis=1).astype(BF)

    q_in.wait()
    q_t = jnp.transpose(q_v[...].astype(F32)) * (hd ** -0.5)
    q_blocks = blocks(q_t)
    col = iota((width, cols), 1)
    for h in range(1, heads):
        col = jnp.where(iota((width, cols), 1) >= h * rows, iota((width, cols), 1) - h * rows, col)
    tile_of = jnp.zeros((width, cols), jnp.int32)
    for t in range(1, tiles):
        tile_of = jnp.where(col >= t * tile, t, tile_of)
    in_tile = jnp.where(iota((width, cols), 0) == tile_of, 1.0, 0.0).astype(BF)
    q_aug = jnp.concatenate([q_blocks, in_tile], axis=0)

    step_rows = min(mix, 256)
    last = [(far0, cap + mix)] if mix <= 256 else [(far0, cap)]
    if mix > 256:
        last += [(mix0 + i, step_rows) for i in range(0, mix, step_rows)]
    first = [(0, rows), (rows, cap)]

    def score(c):
        a, size = c
        keys = jnp.concatenate([kv[a : a + size, :width], bias[a : a + size, :]], axis=1)
        s = mm(keys, q_aug, NN)
        top = jnp.max(s, axis=0, keepdims=True)
        e = jnp.exp(s - top)
        e_ref[a : a + size, :] = e
        return top, jnp.sum(e, axis=0, keepdims=True)

    def mixed_value(c):
        a, size = c
        kvt[:, a : a + size] = jnp.transpose(kv[a : a + size, :])
        return jnp.concatenate(
            [
                mm(
                    kvt[width + h * hd : width + (h + 1) * hd, a : a + size],
                    e_ref[a : a + size, h * rows : (h + 1) * rows].astype(BF),
                    NN,
                )
                for h in range(heads)
            ],
            axis=1,
        )

    def slope(c):
        a, size = c
        dp = mm(kv[a : a + size, width:], g_blocks, NN)
        dp_ref[a : a + size, :] = dp
        return jnp.sum(dp * e_ref[a : a + size, :], axis=0, keepdims=True)

    stats = [score(first[0])]
    sums = [mixed_value(first[0])]
    scatter_near = jnp.where(iota((rows, cap), 0) == near_rows, 1.0, 0.0).astype(BF)
    scatter_far = [jnp.where(iota((rows, cap), 0) == far_rows, 1.0, 0.0).astype(BF)]
    for i in range(groups):
        scatter_far.append(
            jnp.where(iota((rows, cap), 0) == target[i : i + 1, :], 1.0, 0.0).astype(BF)
        )
    scatter_far = jnp.concatenate(scatter_far, axis=1)

    push(kv.at[rows:far0, :], kv.at[rows:far0, :], out_s, near_r, nodes=near).wait_recv()
    stats.append(score(first[1]))
    sums.append(mixed_value(first[1]))

    w_in.wait()
    push(proj.at[: mp - 1], proj.at[: mp - 1], cot_s, cot_r, mp=lax.rem(mm_i + 1, mp)).wait_recv()
    g_t = mm(w_v[...], jnp.concatenate([cot[i] for i in range(mp)], axis=1), NT)
    g_blocks = blocks(g_t.astype(BF).astype(F32))
    slopes = [slope(c) for c in first]

    arrived = push(
        kv.at[far0 : total - blk, :], kv.at[far0 : total - blk, :], out_s, far_r, nodes=far
    )
    arrived.wait_recv()
    for c in last:
        stats.append(score(c))
        slopes.append(slope(c))

    top = functools.reduce(jnp.maximum, [t for t, _ in stats])
    factor = [jnp.exp(t - top) for t, _ in stats]
    inv = 1.0 / sum(f * z for f, (_, z) in zip(factor, stats))
    delta = sum(f * d for f, d in zip(factor, slopes)) * inv
    scale = {c: f * inv for c, f in zip(first + last, factor)}

    def backward(c):
        a, size = c
        p = e_ref[a : a + size, :] * scale[c]
        pb = p.astype(BF)
        ds = (p * (dp_ref[a : a + size, :] - delta)).astype(BF)
        ds_ref[a : a + size, :] = ds
        return mm(ds, q_blocks, NT), mm(pb, g_blocks, NT)

    def to_back(c):
        gk, gv = backward(c)
        a = c[0] - rows
        gback[a : a + c[1], :width] = gk.astype(BF)
        gback[a : a + c[1], width:] = gv.astype(BF)

    def mix_home(d):
        return push(
            gback.at[pl.ds(2 * cap + d * blk, blk), :], ret.at[pl.ds(2 * cap + d * blk, blk), :],
            home_s, home_far_r, nodes=lax.rem(me + n - d, n),
        )

    for c in last:
        to_back(c)
    to_back(first[1])

    def far_home():
        push(
            gback.at[cap : 2 * cap, :], ret.at[cap : 2 * cap, :], home_s, home_far_r, nodes=far
        ).start()

    def near_home():
        push(gback.at[:cap, :], ret.at[:cap, :], home_s, home_near_r, nodes=near).start()


    def send_home(peer):
        d = lax.rem(me - peer + n, n)
        pl.when(d > 0)(lambda: mix_home(d).start())

    send_home(0)
    pl.when(me == n - 1)(far_home)
    pl.when(me < n - 1)(near_home)

    sums += [mixed_value(c) for c in last]
    attn_t = jnp.concatenate(
        [
            sum(
                scale[c][:, h * rows : (h + 1) * rows] * o[:, h * rows : (h + 1) * rows]
                for c, o in zip(first + last, sums)
            )
            for h in range(heads)
        ],
        axis=0,
    )
    attn = jnp.transpose(attn_t).astype(BF)

    def proj_copy(d):
        peer = lax.rem(mm_i + d, mp)
        return push(proj.at[peer], proj_in.at[d - 1], proj_s, proj_r, mp=peer)

    full = mm(attn, w_v[...], NN)
    for i in range(mp):
        proj[i] = full[:, i * width : (i + 1) * width].astype(BF)
    def send_proj(peer):
        d = lax.rem(peer - mm_i + mp, mp)
        pl.when(d > 0)(lambda: proj_copy(d).start())

    send_proj(0)
    for i in range(1, mp):
        send_proj(i)

    pl.when(me == n - 1)(near_home)
    pl.when(me < n - 1)(far_home)
    each(n - 1, lambda j: send_home(j + 1))

    gk, gv = backward(first[0])
    acc = jnp.concatenate([gk, gv], axis=1)
    ret[2 * cap : 2 * cap + blk, :] = gback[2 * cap : 2 * cap + blk, :]

    gq_t = jnp.concatenate(
        [
            mm(kvt[h * hd : (h + 1) * hd, :], ds_ref[:, h * rows : (h + 1) * rows], NN)
            for h in range(heads)
        ],
        axis=0,
    )
    gq_v[...] = jnp.transpose(gq_t * (hd ** -0.5))

    mine = mm(attn, w_v[:, pl.ds(pl.multiple_of(mm_i * width, width), width)], NN)
    push(gback.at[:cap, :], ret.at[:cap, :], home_s, home_near_r, nodes=near).wait_recv()
    acc = acc + mm(scatter_near, ret[:cap, :], NN)

    push(proj.at[: mp - 1], proj_in, proj_s, proj_r, mp=lax.rem(mm_i + 1, mp)).wait_recv()
    for d in range(mp - 1):
        mine = mine + proj_in[d].astype(F32)
    out_v[...] = mine.astype(BF)

    push(
        gback.at[cap : 2 * cap + mix - blk, :], ret.at[cap : 2 * cap + mix - blk, :],
        home_s, home_far_r, nodes=far,
    ).wait_recv()
    acc = acc + mm(scatter_far, ret[cap:, :], NN)
    gk_v[...] = acc[:, :width]
    gv_v[...] = acc[:, width:]
    virt = jnp.sum(ret[2 * cap :, :].astype(F32).reshape(n, blk, 2 * width), axis=0)
    gvk_v[...] = virt[:vn, :width]
    gvv_v[...] = virt[:vn, width:]

    sent = send_buf.at[: 2 * cap + mix - blk, :]
    push(sent, sent, out_s, far_r, nodes=far).wait_send()
    back = gback.at[: 2 * cap + mix - blk, :]
    push(back, back, home_s, far_r, nodes=far).wait_send()
    push(proj_in, proj_in, cot_s, cot_r, mp=lax.rem(mm_i + 1, mp)).wait_send()
    push(proj_in, proj_in, proj_s, proj_r, mp=lax.rem(mm_i + 1, mp)).wait_send()


def hand_over(*refs):
    sem = refs[-1]
    copies = [pltpu.make_async_copy(refs[i], refs[6 + i], sem.at[i]) for i in range(6)]
    for c in copies:
        c.start()
    for c in copies:
        c.wait()


def solution(mesh):
    n, mp = mesh.shape["nodes"], mesh.shape["mp"]
    heads = HEADS // mp

    def step(q, k, v, w, cot, vk, vv, hrows, live, erows, lmask, emask):
        rows, width = q.shape
        cap, slots, vn = hrows.shape[2], erows.shape[2], vk.shape[0]
        blk = -(-(vn + slots) // 16) * 16
        mix = n * blk
        total = rows + 2 * cap + mix
        hbm = pl.BlockSpec(memory_space=pltpu.HBM)
        anywhere = pl.BlockSpec(memory_space=pl.ANY)
        erows = jnp.swapaxes(erows, 1, 2)
        smalls = [pltpu.SMEM(x.shape, jnp.int32) for x in (live, erows, lmask, emask)]
        dma = pltpu.SemaphoreType.DMA
        flops = 2 * total * rows * width * 5
        operands = [
            pltpu.with_memory_space_constraint(x, pltpu.HBM)
            for x in (live, erows, lmask, emask, q, k, v, w, cot, vk, vv, hrows)
        ]
        results = pl.pallas_call(
            functools.partial(kernel, n, mp, heads),
            out_shape=(
                jax.ShapeDtypeStruct((rows, width), BF),
                jax.ShapeDtypeStruct((rows, width), F32),
                jax.ShapeDtypeStruct((rows, width), F32),
                jax.ShapeDtypeStruct((rows, width), F32),
                jax.ShapeDtypeStruct((vn, width), F32),
                jax.ShapeDtypeStruct((vn, width), F32),
            ),
            in_specs=[hbm] * 12,
            out_specs=(pl.BlockSpec(memory_space=pltpu.VMEM),) * 6,
            scratch_shapes=smalls + [
                pltpu.VMEM((rows, width), BF),
                pltpu.VMEM(w.shape, BF),
                pltpu.VMEM((2, vn, width), BF),
                pltpu.VMEM(hrows.shape, jnp.int32),
                pltpu.VMEM((total, 2 * width), BF),
                pltpu.VMEM((mp, rows, width), BF),
                pltpu.VMEM((total, width), BF),
                pltpu.VMEM((2 * cap + mix, rows), BF),
                pltpu.VMEM((2 * cap + mix, 2 * width), BF),
                pltpu.VMEM((2 * width, total), BF),
                pltpu.VMEM((total, heads * rows), F32),
                pltpu.VMEM((total, heads * rows), F32),
                pltpu.VMEM((total, heads * rows), BF),
                pltpu.VMEM((total, heads * rows), BF),
                pltpu.VMEM((2 * cap + mix, 2 * width), BF),
                pltpu.VMEM((2 * cap + mix, 2 * width), BF),
                pltpu.VMEM((mp, rows, width), BF),
                pltpu.VMEM((mp - 1, rows, width), BF),
                dma((10,)),
                pltpu.SemaphoreType.REGULAR((5,)),
                pltpu.SemaphoreType.REGULAR((1,)),
            ] + [dma((1,))] * 10,
            compiler_params=pltpu.CompilerParams(
                collective_id=0, has_side_effects=True, vmem_limit_bytes=40 << 20
            ),
            cost_estimate=pl.CostEstimate(
                flops=flops, transcendentals=total * rows * heads, bytes_accessed=2 << 20
            ),
        )(*operands)
        return pl.pallas_call(
            hand_over,
            out_shape=tuple(jax.ShapeDtypeStruct(x.shape, x.dtype) for x in results),
            in_specs=[anywhere] * 6,
            out_specs=(hbm,) * 6,
            scratch_shapes=[dma((6,))],
            compiler_params=pltpu.CompilerParams(vmem_limit_bytes=4 << 20),
            cost_estimate=pl.CostEstimate(flops=0, transcendentals=0, bytes_accessed=1 << 20),
        )(*results)

    node = P("nodes", "mp")
    return jax.shard_map(
        step,
        mesh=mesh,
        in_specs=(
            node, node, node, P("mp", None), node, node, node,
            P("nodes", None, None), P("nodes", None), P("nodes", None, None),
            P("nodes", None), P("nodes", None),
        ),
        out_specs=(node,) * 6,
        check_vma=False,
    )
```

```python
import functools

import jax
import jax.numpy as jnp
from jax import lax
from jax.experimental import pallas as pl
from jax.experimental.pallas import tpu as pltpu
from jax.sharding import PartitionSpec as P

HEADS = 8
MESH = pl.DeviceIdType.MESH
BF = jnp.bfloat16
F32 = jnp.float32
MASKED = -1e30

NN = (((1,), (0,)), ((), ()))
NT = (((1,), (1,)), ((), ()))
TN = (((0,), (0,)), ((), ()))


def mm(a, b, dims):
    return lax.dot_general(a, b, dims, preferred_element_type=F32)


def iota(shape, axis):
    return lax.broadcasted_iota(jnp.int32, shape, axis)


def each(count, step):
    if count <= 8:
        for d in range(count):
            step(d)
    else:
        pl.loop(0, count)(step)


def kernel(
    n, mp, heads,
    live_hbm, erows_hbm, lmask_hbm, emask_hbm,
    q_hbm, k_hbm, v_hbm, w_hbm, cot_hbm, vk_hbm, vv_hbm, hrows_hbm,
    out_v, gq_v, gk_v, gv_v, gvk_v, gvv_v,
    live, erows, lmask, emask, q_v, w_v, vkv, hrows, kv, cot, bias, picks, send_buf,
    kvt, e_ref, dp_ref, pb_ref, ds_ref, gback, ret, proj, proj_in,
    in_sem, in_nodes, in_mp, near_r, far_r, out_s, cot_s, cot_r, proj_s, proj_r, home_s, home_near_r, home_far_r, home_mix_r,
):
    me = lax.axis_index("nodes")
    mm_i = lax.axis_index("mp")
    rows, width = q_v.shape
    tiles = lmask.shape[0]
    tile = rows // tiles
    cap = hrows.shape[2]
    slots = erows.shape[1]
    vn = vkv.shape[1]
    mix = ret.shape[0] - 2 * cap
    blk = mix // n
    hd = width // heads
    cols = heads * rows
    odd = lax.rem(me, 2)
    left, right = lax.rem(me + n - 1, n), lax.rem(me + 1, n)
    near = jnp.where(odd == 0, right, left)
    far = jnp.where(odd == 0, left, right)
    far0 = rows + cap
    mix0 = rows + 2 * cap
    total = mix0 + mix
    bands = in_nodes.shape[0] - 1
    band = n // bands

    barrier = pltpu.get_barrier_semaphore()

    def greet(sem, **device):
        pl.semaphore_signal(sem, inc=1, device_id=device, device_id_type=MESH)

    half, end = n // 2, n - 1
    pl.loop(me + 1, jnp.where(me >= half, end, n))(lambda j: greet(barrier, nodes=j))
    pl.when(me == end)(lambda: pl.loop(half, end)(lambda j: greet(barrier, nodes=j)))

    def swap(j):
        return j + 1 - 2 * lax.rem(j, 2) if mp % 2 == 0 else j

    spot = swap(mm_i)
    pl.loop(spot + 1, mp)(lambda j: greet(barrier, mp=swap(j)))

    lower = jnp.where(me == end, half, me)
    expected = lower + jnp.where((me >= half) & (me < end), 1, 0)
    mine_in = jnp.where(me == end, bands, me // band)

    def await_all(sem, count):
        pl.when(count > 0)(lambda: pl.semaphore_wait(sem, count))

    def open_up():
        await_all(barrier, expected + spot)
        pl.loop(0, lower)(lambda j: greet(in_nodes.at[mine_in], nodes=j))
        pl.when((me >= half) & (me < end))(lambda: greet(in_nodes.at[mine_in], nodes=end))
        pl.loop(0, spot)(lambda j: greet(in_mp.at[0], mp=swap(j)))

    pl.when(me == end)(open_up)

    def load(i, src, dst):
        return pltpu.make_async_copy(src, dst, in_sem.at[i])

    kv_in = [load(0, k_hbm, kv.at[:rows, :width]), load(0, v_hbm, kv.at[:rows, width:])]
    hrows_in = load(1, hrows_hbm, hrows)
    erows_in = load(2, erows_hbm, erows)
    vkv_in = [load(3, vk_hbm, vkv.at[0]), load(3, vv_hbm, vkv.at[1])]
    cot_in = load(4, cot_hbm, cot.at[mm_i])
    q_in = load(5, q_hbm, q_v)
    w_in = load(6, w_hbm, w_v)
    small = [load(7, live_hbm, live), load(8, lmask_hbm, lmask), load(9, emask_hbm, emask)]
    for c in [erows_in, *kv_in, hrows_in]:
        c.start()

    pl.when(me < end)(open_up)
    for c in [*vkv_in, cot_in, q_in, w_in, *small]:
        c.start()

    groups = mix // cap
    place = iota((groups, cap), 0) * cap + iota((groups, cap), 1)

    def pick_mix(d, target):
        peer = lax.rem(me + d, n)
        for s in range(slots):
            target = jnp.where(place == d * blk + vn + s, erows[0, s, peer], target)
        return target

    erows_in.wait()
    target = jnp.full((groups, cap), -1, jnp.int32)
    if n <= 8:
        for d in range(n):
            target = pick_mix(d, target)
    else:
        target = lax.fori_loop(0, n, pick_mix, target)

    hrows_in.wait()
    near_rows = jnp.where(odd == 0, hrows[0, 0:1, :], hrows[0, 1:2, :])
    far_rows = jnp.where(odd == 0, hrows[0, 1:2, :], hrows[0, 0:1, :])
    wanted = jnp.concatenate([near_rows, far_rows, target], axis=0)
    lines = 2 + groups
    padded = -(-lines // 8) * 8
    columns = jnp.concatenate(
        [wanted.astype(F32), jnp.zeros((padded - lines, cap), F32)], axis=0
    )
    columns = jnp.transpose(columns).astype(jnp.int32)
    lane_p = iota((cap, rows), 1)
    for i in range(lines):
        picks[i * cap : (i + 1) * cap, :] = jnp.where(
            lane_p == columns[:, i : i + 1], 1.0, 0.0
        ).astype(BF)

    load(0, kv.at[:rows, :], kv.at[:rows, :]).wait()
    own = kv[:rows, :]
    taken = mm(picks[...], own, NN)
    load(3, vkv, vkv).wait()
    virt = jnp.concatenate([vkv[0].astype(F32), vkv[1].astype(F32)], axis=1)
    virt = jnp.concatenate([virt, jnp.zeros((blk - vn, 2 * width), F32)], axis=0)
    send_buf[: 2 * cap, :] = taken[: 2 * cap].astype(BF)
    mixed = (taken[2 * cap :].reshape(n, blk, 2 * width) + virt[None]).astype(BF)
    send_buf[2 * cap :, :] = mixed.reshape(mix, 2 * width)
    cot_in.wait()

    def push(src, dst, send, recv, **device):
        return pltpu.make_async_remote_copy(
            src, dst, send.at[0], recv.at[0], device_id=device, device_id_type=MESH
        )

    def mix_copy(d):
        return push(
            send_buf.at[pl.ds(2 * cap + d * blk, blk), :], kv.at[pl.ds(mix0 + d * blk, blk), :],
            out_s, far_r, nodes=lax.rem(me + d, n),
        )

    def cot_copy(d):
        return push(cot.at[mm_i], cot.at[mm_i], cot_s, cot_r, mp=lax.rem(mm_i + d, mp))

    def far_copy():
        part = cap // 4
        for i in range(4):
            push(
                send_buf.at[cap + i * part : cap + (i + 1) * part, :],
                kv.at[far0 + i * part : far0 + (i + 1) * part, :], out_s, far_r, nodes=far,
            ).start()

    def near_copy():
        push(send_buf.at[:cap, :], kv.at[rows:far0, :], out_s, near_r, nodes=near).start()

    def send_mix(peer):
        pl.when(peer != me)(lambda: mix_copy(lax.rem(peer - me + n, n)).start())

    def send_cot():
        await_all(in_mp.at[0], mp - 1 - spot)
        for d in range(1, mp):
            cot_copy(d).start()

    early = me < half
    pl.when(early)(send_cot)
    for g in range(bands):
        if g == bands // 2:

            @pl.when(early)
            def _():
                pl.semaphore_wait(in_nodes.at[bands], 1)
                pl.when(far == end)(far_copy)
                send_mix(end)

        above = jnp.where(me == end, half, me + 1)
        above = jnp.maximum(g * band, above)
        await_all(in_nodes.at[g], min((g + 1) * band, end) - above)
        pl.when((far // band == g) & ((far < end) | (me >= half)))(far_copy)
        pl.when(near // band == g)(near_copy)
        each(min(band, end - g * band), lambda j: send_mix(g * band + j))
    pl.when(me >= half)(lambda: send_mix(end))
    pl.when(me >= half)(send_cot)
    kv[mix0 : mix0 + blk, :] = send_buf[2 * cap : 2 * cap + blk, :]
    for c in small:
        c.wait()

    lane = iota((1, width), 1)

    def per_tile(values):
        result = jnp.zeros(values[0].shape, F32)
        for t in range(tiles):
            result = jnp.where(lane == t, values[t], result)
        return result.astype(BF)

    def flag(x):
        return jnp.where(x > 0, 0.0, MASKED)

    for u in range(tiles):
        bias[u * tile : (u + 1) * tile, :] = per_tile(
            [jnp.full((tile, width), flag(lmask[t, u]), F32) for t in range(tiles)]
        )
    row_c = iota((cap, width), 0)
    for start, side in ((rows, 1 - odd), (far0, odd)):
        bias[start : start + cap, :] = per_tile(
            [
                jnp.where(row_c < live[0, side], flag(lmask[t, tiles + side]), MASKED)
                for t in range(tiles)
            ]
        )
    row_m = iota((blk, width), 0)

    def mix_mask(d):
        source = lax.rem(me + n - d, n)
        values = []
        for t in range(tiles):
            inner = jnp.where(row_m < vn + slots, flag(emask[t, source]), MASKED)
            values.append(jnp.where(row_m < vn, 0.0, inner))
        bias[pl.ds(mix0 + d * blk, blk), :] = per_tile(values)

    each(n, mix_mask)

    feature = iota((width, rows), 0)

    def blocks(x):
        parts = []
        for h in range(heads):
            mine = (feature >= h * hd) & (feature < (h + 1) * hd)
            parts.append(jnp.where(mine, x, 0.0))
        return jnp.concatenate(parts, axis=1).astype(BF)

    q_in.wait()
    q_t = jnp.transpose(q_v[...].astype(F32)) * (hd ** -0.5)
    q_blocks = blocks(q_t)
    col = iota((width, cols), 1)
    for h in range(1, heads):
        col = jnp.where(iota((width, cols), 1) >= h * rows, iota((width, cols), 1) - h * rows, col)
    tile_of = jnp.zeros((width, cols), jnp.int32)
    for t in range(1, tiles):
        tile_of = jnp.where(col >= t * tile, t, tile_of)
    in_tile = jnp.where(iota((width, cols), 0) == tile_of, 1.0, 0.0).astype(BF)
    q_aug = jnp.concatenate([q_blocks, in_tile], axis=0)

    step_rows = min(mix, 256)
    last = [(far0, cap + mix)] if mix <= 256 else [(far0, cap)]
    if mix > 256:
        last += [(mix0 + i, step_rows) for i in range(0, mix, step_rows)]
    first = [(0, rows), (rows, cap)]

    def score(c):
        a, size = c
        keys = jnp.concatenate([kv[a : a + size, :width], bias[a : a + size, :]], axis=1)
        s = mm(keys, q_aug, NN)
        top = jnp.max(s, axis=0, keepdims=True)
        e = jnp.exp(s - top)
        e_ref[a : a + size, :] = e
        return top, jnp.sum(e, axis=0, keepdims=True)

    def mixed_value(c):
        a, size = c
        kvt[:, a : a + size] = jnp.transpose(kv[a : a + size, :])
        return jnp.concatenate(
            [
                mm(
                    kvt[width + h * hd : width + (h + 1) * hd, a : a + size],
                    e_ref[a : a + size, h * rows : (h + 1) * rows].astype(BF),
                    NN,
                )
                for h in range(heads)
            ],
            axis=1,
        )

    def slope(c):
        a, size = c
        dp = mm(kv[a : a + size, width:], g_blocks, NN)
        dp_ref[a : a + size, :] = dp
        return jnp.sum(dp * e_ref[a : a + size, :], axis=0, keepdims=True)

    stats = [score(first[0])]
    sums = [mixed_value(first[0])]
    scatter_near = jnp.where(iota((rows, cap), 0) == near_rows, 1.0, 0.0).astype(BF)
    scatter_far = jnp.where(iota((rows, cap), 0) == far_rows, 1.0, 0.0).astype(BF)
    scatter_mix = []
    for i in range(groups):
        scatter_mix.append(
            jnp.where(iota((rows, cap), 0) == target[i : i + 1, :], 1.0, 0.0).astype(BF)
        )
    scatter_mix = jnp.concatenate(scatter_mix, axis=1)

    push(kv.at[rows:far0, :], kv.at[rows:far0, :], out_s, near_r, nodes=near).wait_recv()
    stats.append(score(first[1]))
    sums.append(mixed_value(first[1]))

    w_in.wait()
    push(proj.at[: mp - 1], proj.at[: mp - 1], cot_s, cot_r, mp=lax.rem(mm_i + 1, mp)).wait_recv()
    g_t = mm(w_v[...], jnp.concatenate([cot[i] for i in range(mp)], axis=1), NT)
    g_blocks = blocks(g_t.astype(BF).astype(F32))
    slopes = [slope(c) for c in first]

    arrived = push(
        kv.at[far0 : total - blk, :], kv.at[far0 : total - blk, :], out_s, far_r, nodes=far
    )
    arrived.wait_recv()
    for c in last:
        stats.append(score(c))
        slopes.append(slope(c))

    top = functools.reduce(jnp.maximum, [t for t, _ in stats])
    factor = [jnp.exp(t - top) for t, _ in stats]
    inv = 1.0 / sum(f * z for f, (_, z) in zip(factor, stats))
    delta = sum(f * d for f, d in zip(factor, slopes)) * inv
    scale = {c: f * inv for c, f in zip(first + last, factor)}

    def backward(c):
        a, size = c
        p = e_ref[a : a + size, :] * scale[c]
        pb = p.astype(BF)
        ds = (p * (dp_ref[a : a + size, :] - delta)).astype(BF)
        ds_ref[a : a + size, :] = ds
        return mm(ds, q_blocks, NT), mm(pb, g_blocks, NT)

    def to_back(c):
        gk, gv = backward(c)
        a = c[0] - rows
        gback[a : a + c[1], :width] = gk.astype(BF)
        gback[a : a + c[1], width:] = gv.astype(BF)

    def mix_home(d):
        return push(
            gback.at[pl.ds(2 * cap + d * blk, blk), :], ret.at[pl.ds(2 * cap + d * blk, blk), :],
            home_s, home_mix_r, nodes=lax.rem(me + n - d, n),
        )

    for c in last:
        to_back(c)
    to_back(first[1])

    def far_home():
        part = cap // 4
        for i in range(4):
            cut = slice(cap + i * part, cap + (i + 1) * part)
            push(gback.at[cut, :], ret.at[cut, :], home_s, home_far_r, nodes=far).start()

    def near_home():
        push(gback.at[:cap, :], ret.at[:cap, :], home_s, home_near_r, nodes=near).start()


    def send_home(peer):
        d = lax.rem(me - peer + n, n)
        pl.when(d > 0)(lambda: mix_home(d).start())

    send_home(0)
    pl.when(me == n - 1)(far_home)
    pl.when(me < n - 1)(near_home)

    @pl.when(me == 0)
    def _():
        far_home()
        each(n - 1, lambda j: send_home(n - 1 - j))


    sums += [mixed_value(c) for c in last]
    attn_t = jnp.concatenate(
        [
            sum(
                scale[c][:, h * rows : (h + 1) * rows] * o[:, h * rows : (h + 1) * rows]
                for c, o in zip(first + last, sums)
            )
            for h in range(heads)
        ],
        axis=0,
    )
    attn = jnp.transpose(attn_t).astype(BF)

    def proj_copy(d):
        peer = lax.rem(mm_i + d, mp)
        return push(proj.at[peer], proj_in.at[d - 1], proj_s, proj_r, mp=peer)

    full = mm(attn, w_v[...], NN)
    for i in range(mp):
        proj[i] = full[:, i * width : (i + 1) * width].astype(BF)
    def send_proj(peer):
        d = lax.rem(peer - mm_i + mp, mp)
        pl.when(d > 0)(lambda: proj_copy(d).start())

    send_proj(0)
    for i in range(1, mp):
        send_proj(i)

    pl.when(me == n - 1)(near_home)
    pl.when((me > 0) & (me < n - 1))(far_home)
    pl.when(me > 0)(lambda: each(n - 1, lambda j: send_home(j + 1)))

    gk, gv = backward(first[0])
    acc = jnp.concatenate([gk, gv], axis=1)
    ret[2 * cap : 2 * cap + blk, :] = gback[2 * cap : 2 * cap + blk, :]

    gq_t = jnp.concatenate(
        [
            mm(kvt[h * hd : (h + 1) * hd, :], ds_ref[:, h * rows : (h + 1) * rows], NN)
            for h in range(heads)
        ],
        axis=0,
    )
    gq_v[...] = jnp.transpose(gq_t * (hd ** -0.5))

    mine = mm(attn, w_v[:, pl.ds(pl.multiple_of(mm_i * width, width), width)], NN)
    push(gback.at[:cap, :], ret.at[:cap, :], home_s, home_near_r, nodes=near).wait_recv()
    acc = acc + mm(scatter_near, ret[:cap, :], NN)

    push(proj.at[: mp - 1], proj_in, proj_s, proj_r, mp=lax.rem(mm_i + 1, mp)).wait_recv()
    for d in range(mp - 1):
        mine = mine + proj_in[d].astype(F32)
    out_v[...] = mine.astype(BF)

    others = slice(2 * cap, 2 * cap + mix - blk)
    push(gback.at[others, :], ret.at[others, :], home_s, home_mix_r, nodes=far).wait_recv()
    acc = acc + mm(scatter_mix, ret[2 * cap :, :], NN)
    virt = jnp.sum(ret[2 * cap :, :].astype(F32).reshape(n, blk, 2 * width), axis=0)
    gvk_v[...] = virt[:vn, :width]
    gvv_v[...] = virt[:vn, width:]

    sent = send_buf.at[: 2 * cap + mix - blk, :]
    push(sent, sent, out_s, far_r, nodes=far).wait_send()
    back = gback.at[: 2 * cap + mix - blk, :]
    push(back, back, home_s, far_r, nodes=far).wait_send()
    push(proj_in, proj_in, cot_s, cot_r, mp=lax.rem(mm_i + 1, mp)).wait_send()
    push(proj_in, proj_in, proj_s, proj_r, mp=lax.rem(mm_i + 1, mp)).wait_send()

    edge = slice(cap, 2 * cap)
    push(gback.at[edge, :], ret.at[edge, :], home_s, home_far_r, nodes=far).wait_recv()
    acc = acc + mm(scatter_far, ret[edge, :], NN)
    gk_v[...] = acc[:, :width]
    gv_v[...] = acc[:, width:]


def hand_over(*refs):
    sem = refs[-1]
    copies = [pltpu.make_async_copy(refs[i], refs[6 + i], sem.at[i]) for i in range(6)]
    for c in copies:
        c.start()
    for c in copies:
        c.wait()


def solution(mesh):
    n, mp = mesh.shape["nodes"], mesh.shape["mp"]
    heads = HEADS // mp

    def step(q, k, v, w, cot, vk, vv, hrows, live, erows, lmask, emask):
        rows, width = q.shape
        cap, slots, vn = hrows.shape[2], erows.shape[2], vk.shape[0]
        blk = -(-(vn + slots) // 16) * 16
        mix = n * blk
        total = rows + 2 * cap + mix
        hbm = pl.BlockSpec(memory_space=pltpu.HBM)
        anywhere = pl.BlockSpec(memory_space=pl.ANY)
        erows = jnp.swapaxes(erows, 1, 2)
        smalls = [pltpu.SMEM(x.shape, jnp.int32) for x in (live, erows, lmask, emask)]
        dma = pltpu.SemaphoreType.DMA
        flops = 2 * total * rows * width * 5
        operands = [
            pltpu.with_memory_space_constraint(x, pltpu.HBM)
            for x in (live, erows, lmask, emask, q, k, v, w, cot, vk, vv, hrows)
        ]
        results = pl.pallas_call(
            functools.partial(kernel, n, mp, heads),
            out_shape=(
                jax.ShapeDtypeStruct((rows, width), BF),
                jax.ShapeDtypeStruct((rows, width), F32),
                jax.ShapeDtypeStruct((rows, width), F32),
                jax.ShapeDtypeStruct((rows, width), F32),
                jax.ShapeDtypeStruct((vn, width), F32),
                jax.ShapeDtypeStruct((vn, width), F32),
            ),
            in_specs=[hbm] * 12,
            out_specs=(pl.BlockSpec(memory_space=pltpu.VMEM),) * 6,
            scratch_shapes=smalls + [
                pltpu.VMEM((rows, width), BF),
                pltpu.VMEM(w.shape, BF),
                pltpu.VMEM((2, vn, width), BF),
                pltpu.VMEM(hrows.shape, jnp.int32),
                pltpu.VMEM((total, 2 * width), BF),
                pltpu.VMEM((mp, rows, width), BF),
                pltpu.VMEM((total, width), BF),
                pltpu.VMEM((2 * cap + mix, rows), BF),
                pltpu.VMEM((2 * cap + mix, 2 * width), BF),
                pltpu.VMEM((2 * width, total), BF),
                pltpu.VMEM((total, heads * rows), F32),
                pltpu.VMEM((total, heads * rows), F32),
                pltpu.VMEM((total, heads * rows), BF),
                pltpu.VMEM((total, heads * rows), BF),
                pltpu.VMEM((2 * cap + mix, 2 * width), BF),
                pltpu.VMEM((2 * cap + mix, 2 * width), BF),
                pltpu.VMEM((mp, rows, width), BF),
                pltpu.VMEM((mp - 1, rows, width), BF),
                dma((10,)),
                pltpu.SemaphoreType.REGULAR((5,)),
                pltpu.SemaphoreType.REGULAR((1,)),
            ] + [dma((1,))] * 11,
            compiler_params=pltpu.CompilerParams(
                collective_id=0, has_side_effects=True, vmem_limit_bytes=40 << 20
            ),
            cost_estimate=pl.CostEstimate(
                flops=flops, transcendentals=total * rows * heads, bytes_accessed=2 << 20
            ),
        )(*operands)
        return pl.pallas_call(
            hand_over,
            out_shape=tuple(jax.ShapeDtypeStruct(x.shape, x.dtype) for x in results),
            in_specs=[anywhere] * 6,
            out_specs=(hbm,) * 6,
            scratch_shapes=[dma((6,))],
            compiler_params=pltpu.CompilerParams(vmem_limit_bytes=4 << 20),
            cost_estimate=pl.CostEstimate(flops=0, transcendentals=0, bytes_accessed=1 << 20),
        )(*results)

    node = P("nodes", "mp")
    return jax.shard_map(
        step,
        mesh=mesh,
        in_specs=(
            node, node, node, P("mp", None), node, node, node,
            P("nodes", None, None), P("nodes", None), P("nodes", None, None),
            P("nodes", None), P("nodes", None),
        ),
        out_specs=(node,) * 6,
        check_vma=False,
    )
```

```python
import functools

import jax
import jax.numpy as jnp
from jax import lax
from jax.experimental import pallas as pl
from jax.experimental.pallas import tpu as pltpu
from jax.sharding import PartitionSpec as P

HEADS = 8
MESH = pl.DeviceIdType.MESH
BF = jnp.bfloat16
F32 = jnp.float32
MASKED = -1e30

NN = (((1,), (0,)), ((), ()))
NT = (((1,), (1,)), ((), ()))
TN = (((0,), (0,)), ((), ()))


def mm(a, b, dims):
    return lax.dot_general(a, b, dims, preferred_element_type=F32)


def iota(shape, axis):
    return lax.broadcasted_iota(jnp.int32, shape, axis)


def each(count, step):
    if count <= 8:
        for d in range(count):
            step(d)
    else:
        pl.loop(0, count)(step)


def kernel(
    n, mp, heads,
    live_hbm, erows_hbm, lmask_hbm, emask_hbm,
    q_hbm, k_hbm, v_hbm, w_hbm, cot_hbm, vk_hbm, vv_hbm, hrows_hbm,
    out_v, gq_v, gk_v, gv_v, gvk_v, gvv_v,
    live, erows, lmask, emask, q_v, w_v, vkv, hrows, kv, cot, bias, picks, send_buf,
    kvt, e_ref, dp_ref, pb_ref, ds_ref, gback, ret, proj, proj_in,
    in_sem, in_nodes, in_mp, near_r, far_r, out_s, cot_s, cot_r, proj_s, proj_r, home_s, home_near_r, home_far_r, home_mix_r,
):
    me = lax.axis_index("nodes")
    mm_i = lax.axis_index("mp")
    rows, width = q_v.shape
    tiles = lmask.shape[0]
    tile = rows // tiles
    cap = hrows.shape[2]
    slots = erows.shape[1]
    vn = vkv.shape[1]
    mix = ret.shape[0] - 2 * cap
    blk = mix // n
    hd = width // heads
    cols = heads * rows
    odd = lax.rem(me, 2)
    left, right = lax.rem(me + n - 1, n), lax.rem(me + 1, n)
    near = jnp.where(odd == 0, right, left)
    far = jnp.where(odd == 0, left, right)
    far0 = rows + cap
    mix0 = rows + 2 * cap
    total = mix0 + mix
    bands = in_nodes.shape[0] - 1
    band = n // bands

    barrier = pltpu.get_barrier_semaphore()

    def greet(sem, **device):
        pl.semaphore_signal(sem, inc=1, device_id=device, device_id_type=MESH)

    half, end = n // 2, n - 1
    pl.loop(me + 1, jnp.where(me >= half, end, n))(lambda j: greet(barrier, nodes=j))
    pl.when(me == end)(lambda: pl.loop(half, end)(lambda j: greet(barrier, nodes=j)))

    def swap(j):
        return j + 1 - 2 * lax.rem(j, 2) if mp % 2 == 0 else j

    spot = swap(mm_i)
    pl.loop(spot + 1, mp)(lambda j: greet(barrier, mp=swap(j)))

    lower = jnp.where(me == end, half, me)
    expected = lower + jnp.where((me >= half) & (me < end), 1, 0)
    mine_in = jnp.where(me == end, bands, me // band)

    def await_all(sem, count):
        pl.when(count > 0)(lambda: pl.semaphore_wait(sem, count))

    def open_up():
        await_all(barrier, expected + spot)
        pl.loop(0, lower)(lambda j: greet(in_nodes.at[mine_in], nodes=j))
        pl.when((me >= half) & (me < end))(lambda: greet(in_nodes.at[mine_in], nodes=end))
        pl.loop(0, spot)(lambda j: greet(in_mp.at[0], mp=swap(j)))

    pl.when(me == end)(open_up)

    def load(i, src, dst):
        return pltpu.make_async_copy(src, dst, in_sem.at[i])

    kv_in = [load(0, k_hbm, kv.at[:rows, :width]), load(0, v_hbm, kv.at[:rows, width:])]
    hrows_in = load(1, hrows_hbm, hrows)
    erows_in = load(2, erows_hbm, erows)
    vkv_in = [load(3, vk_hbm, vkv.at[0]), load(3, vv_hbm, vkv.at[1])]
    cot_in = load(4, cot_hbm, cot.at[mm_i])
    q_in = load(5, q_hbm, q_v)
    w_in = load(6, w_hbm, w_v)
    small = [load(7, live_hbm, live), load(8, lmask_hbm, lmask), load(9, emask_hbm, emask)]
    for c in [erows_in, *kv_in, hrows_in]:
        c.start()

    pl.when(me < end)(open_up)
    for c in [*vkv_in, cot_in, q_in, w_in, *small]:
        c.start()

    groups = mix // cap
    place = iota((groups, cap), 0) * cap + iota((groups, cap), 1)

    def pick_mix(d, target):
        peer = lax.rem(me + d, n)
        for s in range(slots):
            target = jnp.where(place == d * blk + vn + s, erows[0, s, peer], target)
        return target

    erows_in.wait()
    target = jnp.full((groups, cap), -1, jnp.int32)
    if n <= 8:
        for d in range(n):
            target = pick_mix(d, target)
    else:
        target = lax.fori_loop(0, n, pick_mix, target)

    hrows_in.wait()
    near_rows = jnp.where(odd == 0, hrows[0, 0:1, :], hrows[0, 1:2, :])
    far_rows = jnp.where(odd == 0, hrows[0, 1:2, :], hrows[0, 0:1, :])
    wanted = jnp.concatenate([near_rows, far_rows, target], axis=0)
    lines = 2 + groups
    padded = -(-lines // 8) * 8
    columns = jnp.concatenate(
        [wanted.astype(F32), jnp.zeros((padded - lines, cap), F32)], axis=0
    )
    columns = jnp.transpose(columns).astype(jnp.int32)
    lane_p = iota((cap, rows), 1)
    for i in range(lines):
        picks[i * cap : (i + 1) * cap, :] = jnp.where(
            lane_p == columns[:, i : i + 1], 1.0, 0.0
        ).astype(BF)

    load(0, kv.at[:rows, :], kv.at[:rows, :]).wait()
    own = kv[:rows, :]
    taken = mm(picks[...], own, NN)
    load(3, vkv, vkv).wait()
    virt = jnp.concatenate([vkv[0].astype(F32), vkv[1].astype(F32)], axis=1)
    virt = jnp.concatenate([virt, jnp.zeros((blk - vn, 2 * width), F32)], axis=0)
    send_buf[: 2 * cap, :] = taken[: 2 * cap].astype(BF)
    mixed = (taken[2 * cap :].reshape(n, blk, 2 * width) + virt[None]).astype(BF)
    send_buf[2 * cap :, :] = mixed.reshape(mix, 2 * width)
    cot_in.wait()

    def push(src, dst, send, recv, **device):
        return pltpu.make_async_remote_copy(
            src, dst, send.at[0], recv.at[0], device_id=device, device_id_type=MESH
        )

    def mix_copy(d):
        return push(
            send_buf.at[pl.ds(2 * cap + d * blk, blk), :], kv.at[pl.ds(mix0 + d * blk, blk), :],
            out_s, far_r, nodes=lax.rem(me + d, n),
        )

    def cot_copy(d):
        return push(cot.at[mm_i], cot.at[mm_i], cot_s, cot_r, mp=lax.rem(mm_i + d, mp))

    def far_copy():
        part = cap // 4
        for i in range(4):
            push(
                send_buf.at[cap + i * part : cap + (i + 1) * part, :],
                kv.at[far0 + i * part : far0 + (i + 1) * part, :], out_s, far_r, nodes=far,
            ).start()

    def near_copy():
        push(send_buf.at[:cap, :], kv.at[rows:far0, :], out_s, near_r, nodes=near).start()

    def send_mix(peer):
        pl.when(peer != me)(lambda: mix_copy(lax.rem(peer - me + n, n)).start())

    def send_cot():
        await_all(in_mp.at[0], mp - 1 - spot)
        for d in range(1, mp):
            cot_copy(d).start()

    early = me < half
    pl.when(early)(send_cot)
    for g in range(bands):
        if g == bands // 2:

            @pl.when(early)
            def _():
                pl.semaphore_wait(in_nodes.at[bands], 1)
                pl.when(far == end)(far_copy)
                send_mix(end)

        above = jnp.where(me == end, half, me + 1)
        above = jnp.maximum(g * band, above)
        await_all(in_nodes.at[g], min((g + 1) * band, end) - above)
        pl.when((far // band == g) & ((far < end) | (me >= half)))(far_copy)
        pl.when(near // band == g)(near_copy)
        each(min(band, end - g * band), lambda j: send_mix(g * band + j))
    pl.when(me >= half)(lambda: send_mix(end))
    pl.when(me >= half)(send_cot)
    kv[mix0 : mix0 + blk, :] = send_buf[2 * cap : 2 * cap + blk, :]
    for c in small:
        c.wait()

    lane = iota((1, width), 1)

    def per_tile(values):
        result = jnp.zeros(values[0].shape, F32)
        for t in range(tiles):
            result = jnp.where(lane == t, values[t], result)
        return result.astype(BF)

    def flag(x):
        return jnp.where(x > 0, 0.0, MASKED)

    for u in range(tiles):
        bias[u * tile : (u + 1) * tile, :] = per_tile(
            [jnp.full((tile, width), flag(lmask[t, u]), F32) for t in range(tiles)]
        )
    row_c = iota((cap, width), 0)
    for start, side in ((rows, 1 - odd), (far0, odd)):
        bias[start : start + cap, :] = per_tile(
            [
                jnp.where(row_c < live[0, side], flag(lmask[t, tiles + side]), MASKED)
                for t in range(tiles)
            ]
        )
    row_m = iota((blk, width), 0)

    def mix_mask(d):
        source = lax.rem(me + n - d, n)
        values = []
        for t in range(tiles):
            inner = jnp.where(row_m < vn + slots, flag(emask[t, source]), MASKED)
            values.append(jnp.where(row_m < vn, 0.0, inner))
        bias[pl.ds(mix0 + d * blk, blk), :] = per_tile(values)

    each(n, mix_mask)

    feature = iota((width, rows), 0)

    def blocks(x):
        parts = []
        for h in range(heads):
            mine = (feature >= h * hd) & (feature < (h + 1) * hd)
            parts.append(jnp.where(mine, x, 0.0))
        return jnp.concatenate(parts, axis=1).astype(BF)

    q_in.wait()
    q_t = jnp.transpose(q_v[...].astype(F32)) * (hd ** -0.5)
    q_blocks = blocks(q_t)
    col = iota((width, cols), 1)
    for h in range(1, heads):
        col = jnp.where(iota((width, cols), 1) >= h * rows, iota((width, cols), 1) - h * rows, col)
    tile_of = jnp.zeros((width, cols), jnp.int32)
    for t in range(1, tiles):
        tile_of = jnp.where(col >= t * tile, t, tile_of)
    in_tile = jnp.where(iota((width, cols), 0) == tile_of, 1.0, 0.0).astype(BF)
    q_aug = jnp.concatenate([q_blocks, in_tile], axis=0)

    step_rows = min(mix, 256)
    last = [(far0, cap + mix)] if mix <= 256 else [(far0, cap)]
    if mix > 256:
        last += [(mix0 + i, step_rows) for i in range(0, mix, step_rows)]
    first = [(0, rows), (rows, cap)]

    def score(c):
        a, size = c
        keys = jnp.concatenate([kv[a : a + size, :width], bias[a : a + size, :]], axis=1)
        s = mm(keys, q_aug, NN)
        top = jnp.max(s, axis=0, keepdims=True)
        e = jnp.exp(s - top)
        e_ref[a : a + size, :] = e
        return top, jnp.sum(e, axis=0, keepdims=True)

    def mixed_value(c):
        a, size = c
        kvt[:, a : a + size] = jnp.transpose(kv[a : a + size, :])
        return jnp.concatenate(
            [
                mm(
                    kvt[width + h * hd : width + (h + 1) * hd, a : a + size],
                    e_ref[a : a + size, h * rows : (h + 1) * rows].astype(BF),
                    NN,
                )
                for h in range(heads)
            ],
            axis=1,
        )

    def slope(c):
        a, size = c
        dp = mm(kv[a : a + size, width:], g_blocks, NN)
        dp_ref[a : a + size, :] = dp
        return jnp.sum(dp * e_ref[a : a + size, :], axis=0, keepdims=True)

    stats = [score(first[0])]
    sums = [mixed_value(first[0])]
    scatter_near = jnp.where(iota((rows, cap), 0) == near_rows, 1.0, 0.0).astype(BF)
    scatter_far = jnp.where(iota((rows, cap), 0) == far_rows, 1.0, 0.0).astype(BF)
    scatter_mix = []
    for i in range(groups):
        scatter_mix.append(
            jnp.where(iota((rows, cap), 0) == target[i : i + 1, :], 1.0, 0.0).astype(BF)
        )
    scatter_mix = jnp.concatenate(scatter_mix, axis=1)

    push(kv.at[rows:far0, :], kv.at[rows:far0, :], out_s, near_r, nodes=near).wait_recv()
    stats.append(score(first[1]))
    sums.append(mixed_value(first[1]))

    w_in.wait()
    push(proj.at[: mp - 1], proj.at[: mp - 1], cot_s, cot_r, mp=lax.rem(mm_i + 1, mp)).wait_recv()
    g_t = mm(w_v[...], jnp.concatenate([cot[i] for i in range(mp)], axis=1), NT)
    g_blocks = blocks(g_t.astype(BF).astype(F32))
    slopes = [slope(c) for c in first]

    arrived = push(
        kv.at[far0 : total - blk, :], kv.at[far0 : total - blk, :], out_s, far_r, nodes=far
    )
    arrived.wait_recv()
    for c in last:
        stats.append(score(c))
        slopes.append(slope(c))

    top = functools.reduce(jnp.maximum, [t for t, _ in stats])
    factor = [jnp.exp(t - top) for t, _ in stats]
    inv = 1.0 / sum(f * z for f, (_, z) in zip(factor, stats))
    delta = sum(f * d for f, d in zip(factor, slopes)) * inv
    scale = {c: f * inv for c, f in zip(first + last, factor)}

    def backward(c):
        a, size = c
        p = e_ref[a : a + size, :] * scale[c]
        pb = p.astype(BF)
        ds = (p * (dp_ref[a : a + size, :] - delta)).astype(BF)
        ds_ref[a : a + size, :] = ds
        return mm(ds, q_blocks, NT), mm(pb, g_blocks, NT)

    def to_back(c):
        gk, gv = backward(c)
        a = c[0] - rows
        gback[a : a + c[1], :width] = gk.astype(BF)
        gback[a : a + c[1], width:] = gv.astype(BF)

    def mix_home(d):
        return push(
            gback.at[pl.ds(2 * cap + d * blk, blk), :], ret.at[pl.ds(2 * cap + d * blk, blk), :],
            home_s, home_mix_r, nodes=lax.rem(me + n - d, n),
        )

    for c in last:
        to_back(c)
    to_back(first[1])

    def far_home():
        part = cap // 4
        for i in range(4):
            cut = slice(cap + i * part, cap + (i + 1) * part)
            push(gback.at[cut, :], ret.at[cut, :], home_s, home_far_r, nodes=far).start()

    def near_home():
        push(gback.at[:cap, :], ret.at[:cap, :], home_s, home_near_r, nodes=near).start()


    def send_home(peer):
        d = lax.rem(me - peer + n, n)
        pl.when(d > 0)(lambda: mix_home(d).start())

    send_home(0)
    pl.when(me == n - 1)(far_home)
    pl.when(me < n - 1)(near_home)

    @pl.when(me == 0)
    def _():
        far_home()
        each(n - 1, lambda j: send_home(n - 1 - j))


    pl.when(me == n - 1)(near_home)
    pl.when((me > 0) & (me < n - 1))(far_home)
    pl.when(me > 0)(lambda: each(n - 1, lambda j: send_home(j + 1)))
    sums += [mixed_value(c) for c in last]
    attn_t = jnp.concatenate(
        [
            sum(
                scale[c][:, h * rows : (h + 1) * rows] * o[:, h * rows : (h + 1) * rows]
                for c, o in zip(first + last, sums)
            )
            for h in range(heads)
        ],
        axis=0,
    )
    attn = jnp.transpose(attn_t).astype(BF)

    def proj_copy(d):
        peer = lax.rem(mm_i + d, mp)
        return push(proj.at[peer], proj_in.at[d - 1], proj_s, proj_r, mp=peer)

    full = mm(attn, w_v[...], NN)
    for i in range(mp):
        proj[i] = full[:, i * width : (i + 1) * width].astype(BF)
    def send_proj(peer):
        d = lax.rem(peer - mm_i + mp, mp)
        pl.when(d > 0)(lambda: proj_copy(d).start())

    send_proj(0)
    for i in range(1, mp):
        send_proj(i)


    gk, gv = backward(first[0])
    acc = jnp.concatenate([gk, gv], axis=1)
    ret[2 * cap : 2 * cap + blk, :] = gback[2 * cap : 2 * cap + blk, :]

    gq_t = jnp.concatenate(
        [
            mm(kvt[h * hd : (h + 1) * hd, :], ds_ref[:, h * rows : (h + 1) * rows], NN)
            for h in range(heads)
        ],
        axis=0,
    )
    gq_v[...] = jnp.transpose(gq_t * (hd ** -0.5))

    mine = mm(attn, w_v[:, pl.ds(pl.multiple_of(mm_i * width, width), width)], NN)
    push(gback.at[:cap, :], ret.at[:cap, :], home_s, home_near_r, nodes=near).wait_recv()
    acc = acc + mm(scatter_near, ret[:cap, :], NN)

    push(proj.at[: mp - 1], proj_in, proj_s, proj_r, mp=lax.rem(mm_i + 1, mp)).wait_recv()
    for d in range(mp - 1):
        mine = mine + proj_in[d].astype(F32)
    out_v[...] = mine.astype(BF)

    others = slice(2 * cap, 2 * cap + mix - blk)
    push(gback.at[others, :], ret.at[others, :], home_s, home_mix_r, nodes=far).wait_recv()
    acc = acc + mm(scatter_mix, ret[2 * cap :, :], NN)
    virt = jnp.sum(ret[2 * cap :, :].astype(F32).reshape(n, blk, 2 * width), axis=0)
    gvk_v[...] = virt[:vn, :width]
    gvv_v[...] = virt[:vn, width:]

    sent = send_buf.at[: 2 * cap + mix - blk, :]
    push(sent, sent, out_s, far_r, nodes=far).wait_send()
    back = gback.at[: 2 * cap + mix - blk, :]
    push(back, back, home_s, far_r, nodes=far).wait_send()
    push(proj_in, proj_in, cot_s, cot_r, mp=lax.rem(mm_i + 1, mp)).wait_send()
    push(proj_in, proj_in, proj_s, proj_r, mp=lax.rem(mm_i + 1, mp)).wait_send()

    edge = slice(cap, 2 * cap)
    push(gback.at[edge, :], ret.at[edge, :], home_s, home_far_r, nodes=far).wait_recv()
    acc = acc + mm(scatter_far, ret[edge, :], NN)
    gk_v[...] = acc[:, :width]
    gv_v[...] = acc[:, width:]


def hand_over(*refs):
    sem = refs[-1]
    copies = [pltpu.make_async_copy(refs[i], refs[6 + i], sem.at[i]) for i in range(6)]
    for c in copies:
        c.start()
    for c in copies:
        c.wait()


def solution(mesh):
    n, mp = mesh.shape["nodes"], mesh.shape["mp"]
    heads = HEADS // mp

    def step(q, k, v, w, cot, vk, vv, hrows, live, erows, lmask, emask):
        rows, width = q.shape
        cap, slots, vn = hrows.shape[2], erows.shape[2], vk.shape[0]
        blk = -(-(vn + slots) // 16) * 16
        mix = n * blk
        total = rows + 2 * cap + mix
        hbm = pl.BlockSpec(memory_space=pltpu.HBM)
        anywhere = pl.BlockSpec(memory_space=pl.ANY)
        erows = jnp.swapaxes(erows, 1, 2)
        smalls = [pltpu.SMEM(x.shape, jnp.int32) for x in (live, erows, lmask, emask)]
        dma = pltpu.SemaphoreType.DMA
        flops = 2 * total * rows * width * 5
        operands = [
            pltpu.with_memory_space_constraint(x, pltpu.HBM)
            for x in (live, erows, lmask, emask, q, k, v, w, cot, vk, vv, hrows)
        ]
        results = pl.pallas_call(
            functools.partial(kernel, n, mp, heads),
            out_shape=(
                jax.ShapeDtypeStruct((rows, width), BF),
                jax.ShapeDtypeStruct((rows, width), F32),
                jax.ShapeDtypeStruct((rows, width), F32),
                jax.ShapeDtypeStruct((rows, width), F32),
                jax.ShapeDtypeStruct((vn, width), F32),
                jax.ShapeDtypeStruct((vn, width), F32),
            ),
            in_specs=[hbm] * 12,
            out_specs=(pl.BlockSpec(memory_space=pltpu.VMEM),) * 6,
            scratch_shapes=smalls + [
                pltpu.VMEM((rows, width), BF),
                pltpu.VMEM(w.shape, BF),
                pltpu.VMEM((2, vn, width), BF),
                pltpu.VMEM(hrows.shape, jnp.int32),
                pltpu.VMEM((total, 2 * width), BF),
                pltpu.VMEM((mp, rows, width), BF),
                pltpu.VMEM((total, width), BF),
                pltpu.VMEM((2 * cap + mix, rows), BF),
                pltpu.VMEM((2 * cap + mix, 2 * width), BF),
                pltpu.VMEM((2 * width, total), BF),
                pltpu.VMEM((total, heads * rows), F32),
                pltpu.VMEM((total, heads * rows), F32),
                pltpu.VMEM((total, heads * rows), BF),
                pltpu.VMEM((total, heads * rows), BF),
                pltpu.VMEM((2 * cap + mix, 2 * width), BF),
                pltpu.VMEM((2 * cap + mix, 2 * width), BF),
                pltpu.VMEM((mp, rows, width), BF),
                pltpu.VMEM((mp - 1, rows, width), BF),
                dma((10,)),
                pltpu.SemaphoreType.REGULAR((5,)),
                pltpu.SemaphoreType.REGULAR((1,)),
            ] + [dma((1,))] * 11,
            compiler_params=pltpu.CompilerParams(
                collective_id=0, has_side_effects=True, vmem_limit_bytes=40 << 20
            ),
            cost_estimate=pl.CostEstimate(
                flops=flops, transcendentals=total * rows * heads, bytes_accessed=2 << 20
            ),
        )(*operands)
        return pl.pallas_call(
            hand_over,
            out_shape=tuple(jax.ShapeDtypeStruct(x.shape, x.dtype) for x in results),
            in_specs=[anywhere] * 6,
            out_specs=(hbm,) * 6,
            scratch_shapes=[dma((6,))],
            compiler_params=pltpu.CompilerParams(vmem_limit_bytes=4 << 20),
            cost_estimate=pl.CostEstimate(flops=0, transcendentals=0, bytes_accessed=1 << 20),
        )(*results)

    node = P("nodes", "mp")
    return jax.shard_map(
        step,
        mesh=mesh,
        in_specs=(
            node, node, node, P("mp", None), node, node, node,
            P("nodes", None, None), P("nodes", None), P("nodes", None, None),
            P("nodes", None), P("nodes", None),
        ),
        out_specs=(node,) * 6,
        check_vma=False,
    )
```
